32 devices in a mesh: bel: 8 (over z, x), st: 4 (over y, core).
Axes of the slice: x: 2, y: 2, z: 4, core: 2. Of those that a mesh axis runs over, the one named last changes fastest.
Arguments:
- alphas: bfloat16 [512, 12288], P(None, 'st'), may hold values from -120 to 120
- transitions: bfloat16 [6, 12288, 12288], P(None, 'bel', 'st'), may hold values from 0.0009994507 to 10
- observe: bfloat16 [6, 48, 12288], P(None, None, 'st'), may hold values from 0.0019989014 to 0.19921875
- reward: bfloat16 [6, 12288], P(None, 'bel'), may hold values from -1.796875 to 1.796875
- belief_index: int32 [128, 6, 48], P('bel'), may hold values from 0 to 511
- action: int32 [128], replicated, may hold values from 0 to 5
Outputs:
- new_alphas: bfloat16 [128, 12288], P('st', 'bel')
The draws below stay inside these ranges and needn't reach their ends.
Inputs may be any that keep to these rules, and one draw needn't show every extreme that they name: `belief_index`: indices of rows of alphas.
All inputs are finite; a program needn't handle non-finite values.
Results may differ from the reference program's by a relative error of at most 0.0044.
Values may be sent and summed in bfloat16 or wider, within the bound.
A program may use at most 128 MiB of HBM per device.

```python
import math
import jax
import jax.numpy as jnp
from jax import lax

S = 12288
ACTS = 6
O = 48
K = 512
BELIEFS = 128


def with_ends(values, rng, low, largest):
    index_at = [jax.random.randint(jax.random.fold_in(rng, axis), (), 0, length) for axis, length in enumerate(values.shape)]
    main_axis = values.shape.index(max(values.shape))
    neighbour = index_at[:main_axis] + [(index_at[main_axis] + 1) % values.shape[main_axis]] + index_at[main_axis + 1:]
    return values.at[tuple(index_at)].set(low).at[tuple(neighbour)].set(largest)


def block_scale(stream_key, extent, shards, smallest, high):
    loudness, own = 1.0, jax.random.fold_in(stream_key, 6)
    for dim, blocks in shards:
        heights = jnp.exp(jax.random.uniform(jax.random.fold_in(own, dim), (blocks,), jnp.float32, smallest / len(shards), high / len(shards)))
        loudness = loudness * jnp.repeat(heights, extent[dim] // blocks).reshape([-1 if axis == dim else 1 for axis in range(len(extent))])
    return loudness


def gaussian(stream_key, dims, width, most, shards=(), kind=jnp.bfloat16):
    drawn = jax.random.normal(stream_key, dims, jnp.float32) * width
    if len(shards) > 0:
        drawn = block_scale(stream_key, dims, shards, -0.22, 0.18) * drawn
    return jnp.clip(drawn, min=-most, max=most).astype(kind)


def setup_inputs(seed: int = 0) -> dict:
    seeds = jax.random.split(jax.random.key(seed), 7)
    alphas = gaussian(seeds[0], (K, S), 20.0, 120.0, ((1, 4),))
    transitions = jnp.clip(jnp.exp(math.log(10.0) - 9.21089 * jax.random.uniform(seeds[1], (ACTS, S, S), jnp.float32) ** block_scale(seeds[1], (ACTS, S, S), ((1, 8), (2, 4)), -0.2, 0.2)), 0.0009994507, 10.0).astype(jnp.bfloat16)
    observe = jnp.clip(jnp.exp(math.log(0.19921875) - 4.6018058 * jax.random.uniform(seeds[2], (ACTS, O, S), jnp.float32) ** block_scale(seeds[2], (ACTS, O, S), ((2, 4),), -0.2, 0.2)), 0.0019989014, 0.19921875).astype(jnp.bfloat16)
    reward = gaussian(seeds[3], (ACTS, S), 0.3, 1.796875, ((1, 8),))
    belief_index = with_ends(jax.random.randint(seeds[4], (BELIEFS, ACTS, O), 0, K), jax.random.fold_in(seeds[4], 1), 0, K - 1).astype(jnp.int32)
    action = with_ends(jax.random.randint(seeds[5], (BELIEFS,), 0, ACTS), jax.random.fold_in(seeds[5], 1), 0, ACTS - 1).astype(jnp.int32)
    return dict(alphas=alphas, transitions=transitions, observe=observe, reward=reward, belief_index=belief_index, action=action)


discount = 0.95


def mixture_block(alphas, observe, index_rows, action_rows):
    onehot = action_rows[:, None] == jnp.arange(ACTS, dtype=jnp.int32)[None, :]
    chosen = jnp.sum(jnp.where(onehot[:, :, None], index_rows, 0), axis=1).astype(jnp.int32)
    picked = alphas[chosen].astype(jnp.float32)
    weights = observe[action_rows].astype(jnp.float32)
    return jnp.sum(picked * weights, axis=1).astype(jnp.bfloat16)


def grouped_product(rows, acts, weights, block):
    count = rows.shape[0]
    kinds = weights.shape[0]
    blocks = count // block + kinds - 1
    onehot = (acts[:, None] == jnp.arange(kinds, dtype=jnp.int32)[None, :]).astype(jnp.int32)
    totals = jnp.sum(onehot, axis=0).astype(jnp.int32)
    filled = ((totals + block - 1) // block).astype(jnp.int32)
    ends = jnp.cumsum(filled).astype(jnp.int32)
    starts = (ends - filled).astype(jnp.int32)
    before = (jnp.cumsum(onehot, axis=0).astype(jnp.int32) - onehot).astype(jnp.int32)
    rank = jnp.sum(before * onehot, axis=1).astype(jnp.int32)
    first = jnp.sum(onehot * starts[None, :], axis=1).astype(jnp.int32)
    target = (first * block + rank).astype(jnp.int32)
    source = jnp.zeros((blocks * block,), jnp.int32).at[target].set(jnp.arange(count, dtype=jnp.int32))
    padded = rows[source].reshape(blocks, block, rows.shape[1])
    owner = jnp.sum((jnp.arange(blocks, dtype=jnp.int32)[:, None] >= ends[None, :]).astype(jnp.int32), axis=1)
    owner = jnp.minimum(owner, kinds - 1).astype(jnp.int32)

    def one_block(pair):
        part, which = pair
        matrix = lax.dynamic_index_in_dim(weights, which, 0, keepdims=False)
        return lax.dot_general(part, matrix, (((1,), (1,)), ((), ())), preferred_element_type=jnp.float32)

    result = lax.map(one_block, (padded, owner)).reshape(blocks * block, weights.shape[1])
    return result[target]


def reference(alphas, transitions, observe, reward, belief_index, action):
    beliefs = belief_index.shape[0]
    block = math.gcd(beliefs, 64)
    index_blocks = belief_index.reshape(beliefs // block, block, ACTS, O)
    action_blocks = action.reshape(beliefs // block, block)
    mixture = lax.map(lambda pair: mixture_block(alphas, observe, pair[0], pair[1]), (index_blocks, action_blocks))
    mixture = mixture.reshape(beliefs, S)
    carried = grouped_product(mixture, action, transitions, math.gcd(beliefs, 256))
    gained = reward[action].astype(jnp.float32)
    return (gained + (discount / S) * carried).astype(jnp.bfloat16)
```

```python
import functools
import math

import jax
import jax.numpy as jnp
from jax import lax
from jax.experimental import pallas as pl
from jax.experimental.pallas import tpu as pltpu
from jax.sharding import PartitionSpec as P

discount = 0.95
MESH = pl.DeviceIdType.MESH
VMEM_BYTES = 67_043_328


def kernel(
    n_bel,
    n_st,
    scale,
    act_s,
    act_row,
    bi,
    reward,
    alphas_h,
    obs_h,
    w_h,
    out,
    alphas_v,
    obs_v,
    w_v,
    onehot,
    act_col,
    mixf,
    mix,
    terms,
    recv,
    in_sem,
    w_sem,
    ag_send,
    ag_recv,
    rs_send,
    rs_recv,
):
    own, acts, obs = bi.shape
    k_rows = alphas_v.shape[0]
    beliefs, depth = mix.shape
    nj, _, nb, _ = w_v.shape
    out_rows = out.shape[0]
    n_chunk = ag_send.shape[1]
    width = depth // n_chunk
    block = act_row.shape[1]
    half = n_bel // 2

    load_alphas = pltpu.make_async_copy(alphas_h, alphas_v, in_sem.at[0])
    load_obs = pltpu.make_async_copy(obs_h, obs_v, in_sem.at[1])
    load_alphas.start()
    load_obs.start()

    def load_w(j, a):
        return pltpu.make_async_copy(
            w_h.at[a, pl.ds(j * nb, nb), :], w_v.at[j, a], w_sem.at[j, a]
        )

    for j in range(nj):
        for a in range(acts):
            load_w(j, a).start()

    me = lax.axis_index("bel")
    st = lax.axis_index("st")
    odd = lax.rem(me, 2)
    pos = (1 - odd) * (me // 2) + odd * (n_bel - 1 - me // 2)

    def at_pos(p):
        p = lax.rem(p + n_bel, n_bel)
        back = p // half
        return (1 - back) * (2 * p) + back * (2 * (n_bel - 1 - p) + 1)

    right, left = at_pos(pos + 1), at_pos(pos - 1)

    barrier = pltpu.get_barrier_semaphore()
    for neighbour in (right, left):
        pl.semaphore_signal(barrier, inc=1, device_id={"bel": neighbour}, device_id_type=MESH)
    for d in range(1, n_st):
        pl.semaphore_signal(
            barrier, inc=1, device_id={"st": lax.rem(st + d, n_st)}, device_id_type=MESH
        )

    eye = lax.broadcasted_iota(jnp.int32, (block, block), 0) == lax.broadcasted_iota(
        jnp.int32, (block, block), 1
    )
    for r in range(beliefs // block):
        row = act_row[r : r + 1, :].astype(jnp.float32)
        act_col[r * block : (r + 1) * block, :] = jnp.sum(
            jnp.where(eye, row, 0.0), axis=1, keepdims=True
        )
    eye_o = lax.broadcasted_iota(jnp.int32, (obs, obs), 0) == lax.broadcasted_iota(
        jnp.int32, (obs, obs), 1
    )
    lanes = lax.broadcasted_iota(jnp.int32, (obs, k_rows), 1).astype(jnp.float32)
    for i in range(own):
        a = act_s[me * own + i]
        row = bi[i, pl.ds(a, 1), :].astype(jnp.float32)
        col = jnp.sum(jnp.where(eye_o, row, 0.0), axis=1, keepdims=True)
        onehot[i * obs : (i + 1) * obs, :] = jnp.where(lanes == col, 1.0, 0.0).astype(jnp.bfloat16)

    load_alphas.wait()
    load_obs.wait()
    pl.semaphore_wait(barrier, 2 + n_st - 1)

    def shard(src, c):
        return mix.at[
            pl.ds(pl.multiple_of(src * own, own), own), pl.ds(c * width, width)
        ]

    def send(direction, c, hop, src):
        piece = shard(src, c)
        return pltpu.make_async_remote_copy(
            src_ref=piece,
            dst_ref=piece,
            send_sem=ag_send.at[direction, c, hop],
            recv_sem=ag_recv.at[direction, c, hop],
            device_id={"bel": right if direction == 0 else left},
            device_id_type=MESH,
        )

    def hops(direction, c):
        return half if (direction + c) % 2 == 0 else n_bel - 1 - half

    group = math.gcd(own, 4)
    for c in range(n_chunk):
        cols = slice(c * width, (c + 1) * width)

        def one_group(g, carry, cols=cols):
            first = pl.multiple_of(g * (group * obs), group * obs)
            picked = jnp.dot(
                onehot[pl.ds(first, group * obs), :],
                alphas_v[:, cols],
                preferred_element_type=jnp.float32,
            )
            for i in range(group):
                a = act_s[me * own + g * group + i]
                weights = obs_v[a, :, cols].astype(jnp.float32)
                part = picked[i * obs : (i + 1) * obs, :] * weights
                mixf[pl.ds(g * group + i, 1), cols] = jnp.sum(part, axis=0, keepdims=True)
            return carry

        lax.fori_loop(0, own // group, one_group, 0)
        mix[pl.ds(pl.multiple_of(me * own, own), own), cols] = mixf[:, cols].astype(jnp.bfloat16)
        for direction in range(2):
            if hops(direction, c) > 0:
                send(direction, c, 0, me).start()

    most = max(half, n_bel - 1 - half)

    def source(direction, hop):
        return at_pos(pos - 1 - hop) if direction == 0 else at_pos(pos + 1 + hop)

    for hop in range(most):
        for c in range(n_chunk):
            for direction in range(2):
                total = hops(direction, c)
                if hop < total:
                    src = source(direction, hop)
                    send(direction, c, hop, src).wait_recv()
                    if hop + 1 < total:
                        send(direction, c, hop + 1, src).start()

    def rs_copy(j, d):
        peer = lax.rem(st + d, n_st)
        return pltpu.make_async_remote_copy(
            src_ref=terms.at[j, pl.ds(pl.multiple_of(peer * out_rows, out_rows), out_rows), :],
            dst_ref=recv.at[d - 1, j],
            send_sem=rs_send.at[j, d - 1],
            recv_sem=rs_recv.at[j, d - 1],
            device_id={"st": peer},
            device_id_type=MESH,
        )

    def one_column_block(j, carry):
        for a in range(acts):
            load_w(j, a).wait()
        for r in range(beliefs // block):
            rows = slice(r * block, (r + 1) * block)
            which = act_col[rows, :]
            total = jnp.zeros((block, nb), jnp.float32)
            for a in range(acts):
                keep = jnp.where(which == float(a), 1.0, 0.0).astype(jnp.bfloat16)
                total += lax.dot_general(
                    mix[rows, :] * keep,
                    w_v[j, a],
                    (((1,), (1,)), ((), ())),
                    preferred_element_type=jnp.float32,
                )
            terms[j, rows, :] = total
        for d in range(1, n_st):
            rs_copy(j, d).start()
        return carry

    lax.fori_loop(0, nj, one_column_block, 0)

    mine = pl.ds(pl.multiple_of(st * out_rows, out_rows), out_rows)
    which = act_col[mine, :]
    for j in range(nj):
        cols = slice(j * nb, (j + 1) * nb)
        gained = jnp.zeros((out_rows, nb), jnp.float32)
        for a in range(acts):
            gained += jnp.where(
                which == float(a), reward[a : a + 1, cols].astype(jnp.float32), 0.0
            )
        total = terms[j, mine, :]
        for d in range(1, n_st):
            rs_copy(j, d).wait_recv()
            total += recv[d - 1, j]
        out[:, cols] = (gained + scale * total).astype(out.dtype)

    for j in range(nj):
        for d in range(1, n_st):
            rs_copy(j, d).wait_send()
    for direction in range(2):
        for c in range(n_chunk):
            for hop in range(hops(direction, c)):
                src = me if hop == 0 else source(direction, hop - 1)
                send(direction, c, hop, src).wait_send()


def body(n_bel, n_st, alphas, transitions, observe, reward, belief_index, action):
    k_rows, depth = alphas.shape
    acts, states, _ = transitions.shape
    obs = observe.shape[1]
    own = belief_index.shape[0]
    beliefs = action.shape[0]
    out_rows = beliefs // n_st
    block = math.gcd(beliefs, 128)
    nb = 256 if states % 256 == 0 else states
    nj = states // nb
    n_chunk = 4 if n_bel <= 16 else 1
    most = max(n_bel // 2, 1)
    scale = discount / (depth * n_st)
    vmem = pl.BlockSpec(memory_space=pltpu.VMEM)
    hbm = pl.BlockSpec(memory_space=pl.ANY)
    return pl.pallas_call(
        functools.partial(kernel, n_bel, n_st, scale),
        out_shape=jax.ShapeDtypeStruct((out_rows, states), jnp.bfloat16),
        in_specs=[pl.BlockSpec(memory_space=pltpu.SMEM), vmem, vmem, vmem, hbm, hbm, hbm],
        out_specs=vmem,
        scratch_shapes=[
            pltpu.VMEM((k_rows, depth), jnp.bfloat16),
            pltpu.VMEM((acts, obs, depth), jnp.bfloat16),
            pltpu.VMEM((nj, acts, nb, depth), jnp.bfloat16),
            pltpu.VMEM((own * obs, k_rows), jnp.bfloat16),
            pltpu.VMEM((beliefs, 1), jnp.float32),
            pltpu.VMEM((own, depth), jnp.float32),
            pltpu.VMEM((beliefs, depth), jnp.bfloat16),
            pltpu.VMEM((nj, beliefs, nb), jnp.float32),
            pltpu.VMEM((n_st - 1, nj, out_rows, nb), jnp.float32),
            pltpu.SemaphoreType.DMA((2,)),
            pltpu.SemaphoreType.DMA((nj, acts)),
            pltpu.SemaphoreType.DMA((2, n_chunk, most)),
            pltpu.SemaphoreType.DMA((2, n_chunk, most)),
            pltpu.SemaphoreType.DMA((nj, n_st - 1)),
            pltpu.SemaphoreType.DMA((nj, n_st - 1)),
        ],
        compiler_params=pltpu.CompilerParams(
            collective_id=0, has_side_effects=True, vmem_limit_bytes=VMEM_BYTES
        ),
    )(
        action,
        action.reshape(beliefs // block, block),
        belief_index,
        reward,
        alphas,
        observe,
        transitions,
    )


def solution(mesh):
    placed = (
        P(None, "st"),
        P(None, "bel", "st"),
        P(None, None, "st"),
        P(None, "bel"),
        P("bel", None, None),
        P(),
    )
    return jax.shard_map(
        functools.partial(body, mesh.shape["bel"], mesh.shape["st"]),
        mesh=mesh,
        in_specs=placed,
        out_specs=P("st", "bel"),
        check_vma=False,
    )
```

```python
import functools
import math

import jax
import jax.numpy as jnp
from jax import lax
from jax.experimental import pallas as pl
from jax.experimental.pallas import tpu as pltpu
from jax.sharding import PartitionSpec as P

discount = 0.95
MESH = pl.DeviceIdType.MESH
VMEM_BYTES = 67_043_328


def kernel(
    n_bel,
    n_st,
    scale,
    act_s,
    act_row,
    bi,
    reward,
    alphas_h,
    obs_h,
    w_h,
    out,
    alphas_v,
    obs_v,
    w_v,
    onehot,
    act_col,
    mixf,
    mix,
    terms,
    recv,
    in_sem,
    w_sem,
    ag_send,
    ag_recv,
    rs_send,
    rs_recv,
):
    own, acts, obs = bi.shape
    k_rows = alphas_v.shape[0]
    beliefs, depth = mix.shape
    nj, _, nb, _ = w_v.shape
    out_rows = out.shape[0]
    n_chunk = ag_send.shape[1]
    width = depth // n_chunk
    block = act_row.shape[1]
    half = n_bel // 2

    load_alphas = pltpu.make_async_copy(alphas_h, alphas_v, in_sem.at[0])
    load_obs = pltpu.make_async_copy(obs_h, obs_v, in_sem.at[1])
    load_alphas.start()
    load_obs.start()

    def load_w(j, a):
        return pltpu.make_async_copy(
            w_h.at[a, pl.ds(j * nb, nb), :], w_v.at[j, a], w_sem.at[j, a]
        )

    me = lax.axis_index("bel")
    st = lax.axis_index("st")
    odd = lax.rem(me, 2)
    pos = (1 - odd) * (me // 2) + odd * (n_bel - 1 - me // 2)

    def at_pos(p):
        p = lax.rem(p + n_bel, n_bel)
        back = p // half
        return (1 - back) * (2 * p) + back * (2 * (n_bel - 1 - p) + 1)

    right, left = at_pos(pos + 1), at_pos(pos - 1)

    barrier = pltpu.get_barrier_semaphore()
    for neighbour in (right, left):
        pl.semaphore_signal(barrier, inc=1, device_id={"bel": neighbour}, device_id_type=MESH)
    for d in range(1, n_st):
        pl.semaphore_signal(
            barrier, inc=1, device_id={"st": lax.rem(st + d, n_st)}, device_id_type=MESH
        )

    eye = lax.broadcasted_iota(jnp.int32, (block, block), 0) == lax.broadcasted_iota(
        jnp.int32, (block, block), 1
    )
    for r in range(beliefs // block):
        row = act_row[r : r + 1, :].astype(jnp.float32)
        act_col[r * block : (r + 1) * block, :] = jnp.sum(
            jnp.where(eye, row, 0.0), axis=1, keepdims=True
        )
    eye_o = lax.broadcasted_iota(jnp.int32, (obs, obs), 0) == lax.broadcasted_iota(
        jnp.int32, (obs, obs), 1
    )
    lanes = lax.broadcasted_iota(jnp.int32, (obs, k_rows), 1).astype(jnp.float32)
    for i in range(own):
        a = act_s[me * own + i]
        row = bi[i, pl.ds(a, 1), :].astype(jnp.float32)
        col = jnp.sum(jnp.where(eye_o, row, 0.0), axis=1, keepdims=True)
        onehot[i * obs : (i + 1) * obs, :] = jnp.where(lanes == col, 1.0, 0.0).astype(jnp.bfloat16)

    load_alphas.wait()
    load_obs.wait()
    queue = list(range(nj))

    def issue(count):
        for j in queue[:count]:
            for a in range(acts):
                load_w(j, a).start()
        del queue[:count]

    issue((nj + 2) // 3)
    pl.semaphore_wait(barrier, 2 + n_st - 1)

    def shard(src, c):
        return mix.at[
            pl.ds(pl.multiple_of(src * own, own), own), pl.ds(c * width, width)
        ]

    def send(direction, c, hop, src):
        piece = shard(src, c)
        return pltpu.make_async_remote_copy(
            src_ref=piece,
            dst_ref=piece,
            send_sem=ag_send.at[direction, c, hop],
            recv_sem=ag_recv.at[direction, c, hop],
            device_id={"bel": right if direction == 0 else left},
            device_id_type=MESH,
        )

    def hops(direction, c):
        return half if (direction + c) % 2 == 0 else n_bel - 1 - half

    group = math.gcd(own, 4)

    def mixture(c):
        cols = slice(c * width, (c + 1) * width)

        def one_group(g, carry):
            first = pl.multiple_of(g * (group * obs), group * obs)
            picked = jnp.dot(
                onehot[pl.ds(first, group * obs), :],
                alphas_v[:, cols],
                preferred_element_type=jnp.float32,
            )
            for i in range(group):
                a = act_s[me * own + g * group + i]
                weights = obs_v[a, :, cols].astype(jnp.float32)
                part = picked[i * obs : (i + 1) * obs, :] * weights
                mixf[pl.ds(g * group + i, 1), cols] = jnp.sum(part, axis=0, keepdims=True)
            return carry

        lax.fori_loop(0, own // group, one_group, 0)
        mix[pl.ds(pl.multiple_of(me * own, own), own), cols] = mixf[:, cols].astype(jnp.bfloat16)

    most = max(half, n_bel - 1 - half)

    def source(direction, hop):
        return at_pos(pos - 1 - hop) if direction == 0 else at_pos(pos + 1 + hop)

    for step in range(n_chunk + most):
        if step < n_chunk:
            mixture(step)
            for direction in range(2):
                if hops(direction, step) > 0:
                    send(direction, step, 0, me).start()
        issue(1 if step < n_chunk - 1 else nj)
        for c in range(min(step, n_chunk)):
            hop = step - 1 - c
            for direction in range(2):
                total = hops(direction, c)
                if hop < total:
                    src = source(direction, hop)
                    send(direction, c, hop, src).wait_recv()
                    if hop + 1 < total:
                        send(direction, c, hop + 1, src).start()

    def rs_copy(j, d):
        peer = lax.rem(st + d, n_st)
        return pltpu.make_async_remote_copy(
            src_ref=terms.at[j, pl.ds(pl.multiple_of(peer * out_rows, out_rows), out_rows), :],
            dst_ref=recv.at[d - 1, j],
            send_sem=rs_send.at[j, d - 1],
            recv_sem=rs_recv.at[j, d - 1],
            device_id={"st": peer},
            device_id_type=MESH,
        )

    def one_column_block(j, carry):
        for a in range(acts):
            load_w(j, a).wait()
        for r in range(beliefs // block):
            rows = slice(r * block, (r + 1) * block)
            which = act_col[rows, :]
            total = jnp.zeros((nb, block), jnp.float32)
            for a in range(acts):
                keep = jnp.where(which == float(a), 1.0, 0.0).astype(jnp.bfloat16)
                total += lax.dot_general(
                    w_v[j, a],
                    mix[rows, :] * keep,
                    (((1,), (1,)), ((), ())),
                    preferred_element_type=jnp.float32,
                )
            terms[j, rows, :] = total.T
        for d in range(1, n_st):
            rs_copy(j, d).start()
        return carry

    lax.fori_loop(0, nj, one_column_block, 0)

    mine = pl.ds(pl.multiple_of(st * out_rows, out_rows), out_rows)
    which = act_col[mine, :]
    for j in range(nj):
        cols = slice(j * nb, (j + 1) * nb)
        gained = jnp.zeros((out_rows, nb), jnp.float32)
        for a in range(acts):
            gained += jnp.where(
                which == float(a), reward[a : a + 1, cols].astype(jnp.float32), 0.0
            )
        total = terms[j, mine, :]
        for d in range(1, n_st):
            rs_copy(j, d).wait_recv()
            total += recv[d - 1, j]
        out[:, cols] = (gained + scale * total).astype(out.dtype)

    for j in range(nj):
        for d in range(1, n_st):
            rs_copy(j, d).wait_send()
    for direction in range(2):
        for c in range(n_chunk):
            for hop in range(hops(direction, c)):
                src = me if hop == 0 else source(direction, hop - 1)
                send(direction, c, hop, src).wait_send()


def body(n_bel, n_st, alphas, transitions, observe, reward, belief_index, action):
    k_rows, depth = alphas.shape
    acts, states, _ = transitions.shape
    obs = observe.shape[1]
    own = belief_index.shape[0]
    beliefs = action.shape[0]
    out_rows = beliefs // n_st
    block = math.gcd(beliefs, 128)
    nb = 512 if states % 512 == 0 else states
    nj = states // nb
    n_chunk = 4 if n_bel <= 16 else 1
    most = max(n_bel // 2, 1)
    scale = discount / (depth * n_st)
    vmem = pl.BlockSpec(memory_space=pltpu.VMEM)
    hbm = pl.BlockSpec(memory_space=pl.ANY)
    return pl.pallas_call(
        functools.partial(kernel, n_bel, n_st, scale),
        out_shape=jax.ShapeDtypeStruct((out_rows, states), jnp.bfloat16),
        in_specs=[pl.BlockSpec(memory_space=pltpu.SMEM), vmem, vmem, vmem, hbm, hbm, hbm],
        out_specs=vmem,
        scratch_shapes=[
            pltpu.VMEM((k_rows, depth), jnp.bfloat16),
            pltpu.VMEM((acts, obs, depth), jnp.bfloat16),
            pltpu.VMEM((nj, acts, nb, depth), jnp.bfloat16),
            pltpu.VMEM((own * obs, k_rows), jnp.bfloat16),
            pltpu.VMEM((beliefs, 1), jnp.float32),
            pltpu.VMEM((own, depth), jnp.float32),
            pltpu.VMEM((beliefs, depth), jnp.bfloat16),
            pltpu.VMEM((nj, beliefs, nb), jnp.float32),
            pltpu.VMEM((n_st - 1, nj, out_rows, nb), jnp.float32),
            pltpu.SemaphoreType.DMA((2,)),
            pltpu.SemaphoreType.DMA((nj, acts)),
            pltpu.SemaphoreType.DMA((2, n_chunk, most)),
            pltpu.SemaphoreType.DMA((2, n_chunk, most)),
            pltpu.SemaphoreType.DMA((nj, n_st - 1)),
            pltpu.SemaphoreType.DMA((nj, n_st - 1)),
        ],
        compiler_params=pltpu.CompilerParams(
            collective_id=0, has_side_effects=True, vmem_limit_bytes=VMEM_BYTES
        ),
    )(
        action,
        action.reshape(beliefs // block, block),
        belief_index,
        reward,
        alphas,
        observe,
        transitions,
    )


def solution(mesh):
    placed = (
        P(None, "st"),
        P(None, "bel", "st"),
        P(None, None, "st"),
        P(None, "bel"),
        P("bel", None, None),
        P(),
    )
    return jax.shard_map(
        functools.partial(body, mesh.shape["bel"], mesh.shape["st"]),
        mesh=mesh,
        in_specs=placed,
        out_specs=P("st", "bel"),
        check_vma=False,
    )
```
